32 devices in a mesh: dp: 8 (over z, x), tensor: 4 (over y, core).
Axes of the slice: x: 2, y: 2, z: 4, core: 2. Of those that a mesh axis runs over, the one named last changes fastest.
Arguments:
- gradients: bfloat16 [8, 4096, 4096], P('dp', None, 'tensor'), may hold values from -300 to 300
- feedback: bfloat16 [8, 4096, 4096], P('dp', None, 'tensor'), may hold values from -12 to 12
- warm_start: float32 [4096, 64], P('tensor'), may hold values from -0.09375 to 0.09375
Outputs:
- projected: float32 [4096, 64], P('tensor')
- refreshed: float32 [4096, 64], P('tensor')
- decompressed: bfloat16 [4096, 4096], P(None, 'tensor')
The draws below stay inside these ranges and needn't reach their ends.
All inputs are finite; a program needn't handle non-finite values.
Results may differ from the reference program's by a relative error of at most 0.001.
Values sent between devices are 32-bit elements; how exact they have to be, the bound alone decides.
A program may use at most 128 MiB of HBM per device.

```python
import jax
import jax.numpy as jnp
from jax import lax

D = 4096
R = 64
N_DP = 8


def draw_gradients(key, part):
    subkeys = jax.random.split(key, 3)
    row_scale = jnp.exp(jax.random.uniform(subkeys[0], (D,), jnp.float32) * jnp.log(10.0))
    col_scale = jnp.exp(jax.random.uniform(subkeys[1], (D,), jnp.float32) * jnp.log(10.0))
    position = jnp.arange(D, dtype=jnp.float32) / (D - 1)
    rising = 1.0 + 2.0 * position
    pattern = jax.random.truncated_normal(subkeys[2], -6.0, 6.0, (N_DP, D, D), jnp.float32)
    values = 0.15 * pattern * (row_scale * rising)[None, :, None] * col_scale[None, None, :]
    return values.astype(jnp.bfloat16)


def block_levels(stream_key, dims, cuts, smallest, high):
    def one(dim, blocks):
        steps = jax.random.uniform(jax.random.fold_in(jax.random.fold_in(stream_key, 6), dim), (blocks,), jnp.float32, smallest / len(cuts), high / len(cuts))
        return jnp.repeat(jnp.exp(steps), dims[dim] // blocks).reshape((-1,) + (1,) * (len(dims) - dim - 1))

    level = one(*cuts[0])
    for cut in cuts[1:]:
        level = level * one(*cut)
    return level


def bell_draw(stream_key, dims, deviation, limit, shards=(), held_as=jnp.bfloat16):
    factor_of = block_levels(stream_key, dims, shards, -0.22, 0.18) if shards else 1.0
    drawn = jax.random.normal(stream_key, dims, jnp.float32) * deviation * factor_of
    return jnp.minimum(jnp.maximum(drawn, -limit), limit).astype(held_as)


def setup_inputs(seed: int = 0) -> dict:
    splits = jax.random.split(jax.random.key(seed), 4)
    return {
        "gradients": draw_gradients(jax.random.fold_in(splits[3], 71), 0),
        "feedback": bell_draw(splits[1], (N_DP, D, D), 2.0, 12.0, ((0, 8), (2, 4))),
        "warm_start": bell_draw(splits[2], (D, R), D ** -0.5, 0.09375, ((0, 4),), jnp.float32),
    }


HIGHEST = lax.Precision.HIGHEST

def reference(gradients, feedback, warm_start):

    def add_left(running, pieces):
        corrected = pieces[0].astype(jnp.float32) + pieces[1].astype(jnp.float32)
        return (running + jnp.dot(corrected, warm_start, precision=HIGHEST), None)
    summed, _ = lax.scan(add_left, jnp.zeros((D, R), jnp.float32), (gradients, feedback))
    projected = summed / N_DP
    gram_matrix = jnp.dot(projected.T, projected, precision=HIGHEST)
    factor = jnp.linalg.cholesky(gram_matrix)
    basis = lax.linalg.triangular_solve(factor, projected, left_side=False, lower=True, transpose_a=True)

    def add_right(running, pieces):
        corrected = pieces[0].astype(jnp.float32) + pieces[1].astype(jnp.float32)
        return (running + jnp.dot(corrected.T, basis, precision=HIGHEST), None)
    total, _ = lax.scan(add_right, jnp.zeros((D, R), jnp.float32), (gradients, feedback))
    refreshed = total / N_DP
    decompressed = jnp.dot(basis, refreshed.T, precision=HIGHEST).astype(jnp.bfloat16)
    return (projected, refreshed, decompressed)
```

```python
import functools

import jax
import jax.numpy as jnp
from jax import lax
from jax.experimental import pallas as pl
from jax.experimental.pallas import tpu as pltpu
from jax.sharding import PartitionSpec as P

MESH = pl.DeviceIdType.MESH
LANES = 128
SUBLANES = 8
MAX_CHUNKS = 4
BLOCK = 256


def pieces(x):
    high = x.astype(jnp.bfloat16)
    rest = x - high.astype(jnp.float32)
    middle = rest.astype(jnp.bfloat16)
    low = (rest - middle.astype(jnp.float32)).astype(jnp.bfloat16)
    return high, middle, low


def fold(x, rank):
    return x[:rank] + x[rank : 2 * rank] + x[2 * rank :]


def inverse_factor(gram, rank):
    row = lax.broadcasted_iota(jnp.int32, (rank, rank), 0)
    column = lax.broadcasted_iota(jnp.int32, (rank, rank), 1)
    both = jnp.concatenate([gram, jnp.where(row == column, 1.0, 0.0).astype(jnp.float32)], axis=1)
    below = lax.broadcasted_iota(jnp.int32, (rank, 1), 0)
    for k in range(rank - 1):
        pivot = both[k : k + 1, k : k + 1]
        scaled = both[k : k + 1, :] * (1.0 / pivot)
        both = both - jnp.where(below > k, both[:, k : k + 1], 0.0) * scaled
    diagonal = jnp.sum(jnp.where(row == column, both[:, :rank], 0.0), axis=1, keepdims=True)
    return both[:, rank:] * (1.0 / jnp.sqrt(diagonal))


def sum_kernel(
    members, tensors, chunks,
    g_hbm, f_hbm, w_ref, own_ref, basis_ref, right_ref,
    g_ref, f_ref, w3_ref, p3_ref, part, acc_core, acc_y, full, recv_core, recv_y, recv_dp,
    right_part, right_full, recv_right, macc, gram_ref,
    load_sem, core_s, core_r, y_s, y_r, dp_s, dp_r, gd_s, gd_r, gy_s, gy_r, gc_s, gc_r,
    ms_s, ms_r, mg_s, mg_r,
):
    depth, width = g_hbm.shape
    rank = w_ref.shape[1]
    ys = tensors // 2
    columns = depth // chunks
    rows = part.shape[0] // chunks
    half, quarter = rows // 2, rows // 2 // ys
    piece = quarter // members
    me = lax.axis_index("dp")
    mine = lax.axis_index("tensor")
    y, core = lax.div(mine, 2), lax.rem(mine, 2)
    partner = y * 2 + (1 - core)

    def member(k):
        return lax.rem(me + k, members)

    def along(k):
        return lax.rem(y + k, ys)

    def dp_device(k):
        return {"dp": member(k), "tensor": mine}

    def y_device(k):
        return {"dp": me, "tensor": along(k) * 2 + core}

    core_device = {"dp": me, "tensor": partner}

    def at(start, size):
        return pl.ds(pl.multiple_of(start, SUBLANES), size)

    def remote(source, target, send, receive, device):
        copy = pltpu.make_async_remote_copy(
            src_ref=source, dst_ref=target, send_sem=send, recv_sem=receive,
            device_id=device, device_id_type=MESH,
        )
        copy.start()
        return copy

    loads = []
    for j in range(chunks):
        here = pl.ds(j * columns, columns)
        pair = [
            pltpu.make_async_copy(g_hbm.at[here], g_ref.at[here], load_sem.at[j, 0]),
            pltpu.make_async_copy(f_hbm.at[here], f_ref.at[here], load_sem.at[j, 1]),
        ]
        for copy in pair:
            copy.start()
        loads.append(pair)

    barrier = pltpu.get_barrier_semaphore()
    partners = [core_device] + [y_device(k) for k in range(1, ys)] + [dp_device(k) for k in range(1, members)]
    for device in partners:
        pl.semaphore_signal(barrier, inc=1, device_id=device, device_id_type=MESH)

    for i, w in enumerate(pieces(w_ref[...].T)):
        w3_ref[i * rank : (i + 1) * rank, :] = w
    pl.semaphore_wait(barrier, len(partners))

    sends = []
    state = [dict() for _ in range(chunks)]

    def project(j):
        for copy in loads[j]:
            copy.wait()
        for b in range(columns // BLOCK):
            here = pl.ds(j * columns + b * BLOCK, BLOCK)
            dims = (((1,), (1,)), ((), ()))
            value = lax.dot_general(w3_ref[...], g_ref[here, :], dims, preferred_element_type=jnp.float32)
            value += lax.dot_general(w3_ref[...], f_ref[here, :], dims, preferred_element_type=jnp.float32)
            value = fold(value, rank)
            for i in range(BLOCK // LANES):
                first = j * rows + (b * (BLOCK // LANES) + i) * rank
                part[first : first + rank, :] = value[:, i * LANES : (i + 1) * LANES]
        state[j]["core"] = remote(
            part.at[at(j * rows + (1 - core) * half, half)], recv_core.at[pl.ds(j * half, half)],
            core_s.at[j], core_r.at[j], core_device,
        )

    def add_core(j):
        copy = state[j]["core"]
        copy.wait_recv()
        sends.append(copy)
        acc_core[j * half : (j + 1) * half, :] = (
            part[at(j * rows + core * half, half), :] + recv_core[j * half : (j + 1) * half, :]
        )
        state[j]["y"] = [
            remote(
                acc_core.at[at(j * half + along(k) * quarter, quarter)], recv_y.at[j, k],
                y_s.at[j, k], y_r.at[j, k], y_device(k),
            )
            for k in range(1, ys)
        ]

    def add_y(j):
        total = acc_core[at(j * half + y * quarter, quarter), :]
        for k, copy in enumerate(state[j]["y"], 1):
            copy.wait_recv()
            sends.append(copy)
            total += recv_y[j, k]
        acc_y[j * quarter : (j + 1) * quarter, :] = total
        state[j]["dp"] = [
            remote(
                acc_y.at[at(j * quarter + member(k) * piece, piece)], recv_dp.at[j, k],
                dp_s.at[j, k], dp_r.at[j, k], dp_device(k),
            )
            for k in range(1, members)
        ]

    def add_dp(j):
        total = acc_y[at(j * quarter + me * piece, piece), :]
        for k, copy in enumerate(state[j]["dp"], 1):
            copy.wait_recv()
            sends.append(copy)
            total += recv_dp[j, k]
        here = at(j * rows + core * half + y * quarter + me * piece, piece)
        full[here, :] = total * (1.0 / members)
        state[j]["gd"] = [
            remote(full.at[here], full.at[here], gd_s.at[j, k], gd_r.at[j, k], dp_device(k))
            for k in range(1, members)
        ]

    def gather_y(j):
        for copy in state[j]["gd"]:
            copy.wait_recv()
            sends.append(copy)
        here = at(j * rows + core * half + y * quarter, quarter)
        state[j]["gy"] = [
            remote(full.at[here], full.at[here], gy_s.at[j, k], gy_r.at[j, k], y_device(k))
            for k in range(1, ys)
        ]

    def gather_core(j):
        for copy in state[j]["gy"]:
            copy.wait_recv()
            sends.append(copy)
        here = at(j * rows + core * half, half)
        state[j]["gc"] = remote(full.at[here], full.at[here], gc_s.at[j], gc_r.at[j], core_device)

    def multiply(j):
        copy = state[j]["gc"]
        copy.wait_recv()
        sends.append(copy)
        for i in range(columns // LANES):
            first = j * rows + i * rank
            for q, p in enumerate(pieces(full[first : first + rank, :])):
                p3_ref[q * rank : (q + 1) * rank, i * LANES : (i + 1) * LANES] = p
        p3 = p3_ref[...]
        square = lax.dot_general(p3, p3, (((1,), (1,)), ((), ())), preferred_element_type=jnp.float32)
        square = fold(square, rank)
        square = square[:, :rank] + square[:, rank : 2 * rank] + square[:, 2 * rank :]
        gram_ref[...] = square if j == 0 else gram_ref[...] + square
        here = pl.ds(j * columns, columns)
        for b in range(width // BLOCK):
            cols = slice(b * BLOCK, (b + 1) * BLOCK)
            value = jnp.dot(p3_ref[...], g_ref[here, cols], preferred_element_type=jnp.float32)
            value += jnp.dot(p3_ref[...], f_ref[here, cols], preferred_element_type=jnp.float32)
            value = fold(value, rank)
            macc[:, cols] = value if j == 0 else macc[:, cols] + value

    stages = [project, add_core, add_y, add_dp, gather_y, gather_core, multiply]
    for step in range(chunks + len(stages) - 1):
        for s in reversed(range(len(stages))):
            if 0 <= step - s < chunks:
                stages[s](step - s)

    groups = width // LANES
    for i in range(groups):
        right_part[i * rank : (i + 1) * rank, :] = macc[:, i * LANES : (i + 1) * LANES]
    share = groups * rank // members
    copies = [
        remote(
            right_part.at[at(member(k) * share, share)], recv_right.at[k],
            ms_s.at[k], ms_r.at[k], dp_device(k),
        )
        for k in range(1, members)
    ]
    inverse = inverse_factor(gram_ref[...], rank)
    total = right_part[at(me * share, share), :]
    for k, copy in enumerate(copies, 1):
        copy.wait_recv()
        sends.append(copy)
        total += recv_right[k]
    here = at(me * share, share)
    right_full[here, :] = total * (1.0 / members)
    copies = [
        remote(right_full.at[here], right_full.at[here], mg_s.at[k], mg_r.at[k], dp_device(k))
        for k in range(1, members)
    ]

    for i in range(depth // LANES):
        value = jnp.dot(
            inverse, full[i * rank : (i + 1) * rank, :],
            precision=lax.Precision.HIGHEST, preferred_element_type=jnp.float32,
        )
        high, middle, _ = pieces(value)
        cols = slice(i * LANES, (i + 1) * LANES)
        basis_ref[:rank, cols] = high
        basis_ref[rank : 2 * rank, cols] = middle
        basis_ref[2 * rank :, cols] = high
    own_ref[...] = full[at(mine * (groups * rank), groups * rank), :]

    for copy in copies:
        copy.wait_recv()
        sends.append(copy)
    for i in range(groups):
        right_ref[:, i * LANES : (i + 1) * LANES] = jnp.dot(
            inverse, right_full[i * rank : (i + 1) * rank, :],
            precision=lax.Precision.HIGHEST, preferred_element_type=jnp.float32,
        )
    for copy in sends:
        copy.wait_send()


def expand_kernel(own_ref, basis_ref, right_ref, projected_ref, refreshed_ref, out_ref, r3_ref):
    rank, width = right_ref.shape

    @pl.when(pl.program_id(0) == 0)
    def _():
        high, middle, _ = pieces(right_ref[...])
        r3_ref[:rank] = high
        r3_ref[rank : 2 * rank] = high
        r3_ref[2 * rank :] = middle
        refreshed_ref[...] = right_ref[...].T
        for i in range(width // LANES):
            projected_ref[i * LANES : (i + 1) * LANES, :] = own_ref[i * rank : (i + 1) * rank, :].T

    out_ref[...] = lax.dot_general(
        basis_ref[...], r3_ref[...], (((0,), (0,)), ((), ())), preferred_element_type=jnp.float32
    ).astype(out_ref.dtype)


def on_device(members, tensors, gradients, feedback, warm_start):
    _, depth, width = gradients.shape
    rank = warm_start.shape[1]
    total_rows = depth * rank // LANES
    chunks = max(1, min(MAX_CHUNKS, total_rows // (SUBLANES * members * tensors)))
    columns = depth // chunks
    rows = total_rows // chunks
    half = rows // 2
    ys = tensors // 2
    quarter = half // ys
    piece = quarter // members
    groups = width // LANES
    share = groups * rank // members
    f32, bf16 = jnp.float32, jnp.bfloat16
    dma = pltpu.SemaphoreType.DMA
    vmem = pl.BlockSpec(memory_space=pltpu.VMEM)
    own, basis, right = pl.pallas_call(
        functools.partial(sum_kernel, members, tensors, chunks),
        out_shape=(
            jax.ShapeDtypeStruct((groups * rank, LANES), f32),
            jax.ShapeDtypeStruct((3 * rank, depth), bf16),
            jax.ShapeDtypeStruct((rank, width), f32),
        ),
        in_specs=[pl.BlockSpec(memory_space=pl.ANY)] * 2 + [vmem],
        out_specs=(vmem, vmem, vmem),
        scratch_shapes=[
            pltpu.VMEM((depth, width), bf16),
            pltpu.VMEM((depth, width), bf16),
            pltpu.VMEM((3 * rank, width), bf16),
            pltpu.VMEM((3 * rank, columns), bf16),
            pltpu.VMEM((total_rows, LANES), f32),
            pltpu.VMEM((total_rows // 2, LANES), f32),
            pltpu.VMEM((total_rows // 2 // ys, LANES), f32),
            pltpu.VMEM((total_rows, LANES), f32),
            pltpu.VMEM((total_rows // 2, LANES), f32),
            pltpu.VMEM((chunks, ys, quarter, LANES), f32),
            pltpu.VMEM((chunks, members, piece, LANES), f32),
            pltpu.VMEM((groups * rank, LANES), f32),
            pltpu.VMEM((groups * rank, LANES), f32),
            pltpu.VMEM((members, share, LANES), f32),
            pltpu.VMEM((rank, width), f32),
            pltpu.VMEM((rank, rank), f32),
            dma((chunks, 2)),
            dma((chunks,)), dma((chunks,)),
            dma((chunks, ys)), dma((chunks, ys)),
            dma((chunks, members)), dma((chunks, members)),
            dma((chunks, members)), dma((chunks, members)),
            dma((chunks, ys)), dma((chunks, ys)),
            dma((chunks,)), dma((chunks,)),
            dma((members,)), dma((members,)),
            dma((members,)), dma((members,)),
        ],
        compiler_params=pltpu.CompilerParams(
            collective_id=0, has_side_effects=True, vmem_limit_bytes=48 * 2**20
        ),
    )(gradients[0], feedback[0], warm_start)

    block = min(512, depth)
    return pl.pallas_call(
        expand_kernel,
        grid=(depth // block,),
        out_shape=(
            jax.ShapeDtypeStruct((width, rank), f32),
            jax.ShapeDtypeStruct((width, rank), f32),
            jax.ShapeDtypeStruct((depth, width), bf16),
        ),
        in_specs=[
            pl.BlockSpec((groups * rank, LANES), lambda i: (0, 0)),
            pl.BlockSpec((3 * rank, block), lambda i: (0, i)),
            pl.BlockSpec((rank, width), lambda i: (0, 0)),
        ],
        out_specs=(
            pl.BlockSpec((width, rank), lambda i: (0, 0)),
            pl.BlockSpec((width, rank), lambda i: (0, 0)),
            pl.BlockSpec((block, width), lambda i: (i, 0)),
        ),
        scratch_shapes=[pltpu.VMEM((3 * rank, width), bf16)],
        compiler_params=pltpu.CompilerParams(dimension_semantics=("arbitrary",)),
    )(own, basis, right)


def solution(mesh):
    return jax.shard_map(
        functools.partial(on_device, mesh.shape["dp"], mesh.shape["tensor"]),
        mesh=mesh,
        in_specs=(P("dp", None, "tensor"), P("dp", None, "tensor"), P("tensor", None)),
        out_specs=(P("tensor", None), P("tensor", None), P(None, "tensor")),
        check_vma=False,
    )
```
